32 devices in a mesh: dp: 8 (over z, x), tensor: 4 (over y, core).
Axes of the slice: x: 2, y: 2, z: 4, core: 2. Of those that a mesh axis runs over, the one named last changes fastest.
Arguments:
- out_grad: bfloat16 [1024, 5120], P('dp'), may hold values from -6 to 6
- gate_act: bfloat16 [1024, 25600], P('dp', 'tensor'), may hold values from -6 to 6
- up_act: bfloat16 [1024, 25600], P('dp', 'tensor'), may hold values from -6 to 6
- codes: int32 [5120, 25600], P('dp', 'tensor'), may hold values from 0 to 15
- zero_points: int32 [5120, 400], P('dp', 'tensor'), may hold values from 0 to 15
- scales: float32 [5120, 400], P('dp', 'tensor'), may hold values from 0.0009782797 to 0.003913119
- rotation: bfloat16 [1600, 1600], replicated, may hold values from -0.15625 to 0.15625
Outputs:
- grad_gate: bfloat16 [1024, 25600], P('dp', 'tensor')
- grad_up: bfloat16 [1024, 25600], P('dp', 'tensor')
- log_scale_grad: float32 [5120, 400], P('dp', 'tensor')
The draws below stay inside these ranges and needn't reach their ends.
All inputs are finite; a program needn't handle non-finite values.
Results may differ from the reference program's by a relative error of at most 0.011.
Values may be sent and summed in bfloat16 or wider, within the bound.
No kernel may reach another device: no remote copies, remote signals or barrier semaphores. Data moves between devices by JAX's collectives and lax.ppermute only.
A program may use at most 128 MiB of HBM per device.

```python
import math
import jax
import jax.numpy as jnp
from jax import lax

D = 5120
FF = 25600
BLOCK = 1600
GROUP = 64
TOKENS = 1024
HAD = 16
GROUPS = 400


def plant(result, rng, least, largest):
    index_at = [jax.random.randint(jax.random.fold_in(rng, axis), (), 0, length) for axis, length in enumerate(result.shape)]
    widest = result.shape.index(max(result.shape))
    beside = index_at[:widest] + [(index_at[widest] + 1) % result.shape[widest]] + index_at[widest + 1:]
    return result.at[tuple(index_at)].set(least).at[tuple(beside)].set(largest)


def steps_of(stream_key, shape, split, low, top_value):
    gain = 1.0
    for axis_at, parts in split:
        heights = jax.random.uniform(jax.random.fold_in(jax.random.fold_in(stream_key, 6), axis_at), (parts,), jnp.float32, low / len(split), top_value / len(split))
        gain = gain * jnp.repeat(jnp.exp(heights), shape[axis_at] // parts).reshape((-1,) + (1,) * (len(shape) - 1 - axis_at))
    return gain


def scatter_about(stream_key, extent, scale, reach, pieces=(), kind=jnp.bfloat16):
    array = scale * jax.random.normal(stream_key, extent, jnp.float32)
    if pieces:
        array = array * steps_of(stream_key, extent, pieces, -0.22, 0.18)
    return jnp.clip(array, -reach, reach).astype(kind)


def setup_inputs(seed: int = 0) -> dict:
    key_of = jax.random.split(jax.random.key(seed), 8)
    return {
        "out_grad": scatter_about(key_of[0], (TOKENS, D), 1.0, 6.0, ((0, 8),)),
        "gate_act": scatter_about(key_of[1], (TOKENS, FF), 1.0, 6.0, ((0, 8), (1, 4))),
        "up_act": scatter_about(key_of[2], (TOKENS, FF), 1.0, 6.0, ((0, 8), (1, 4))),
        "codes": plant(jax.random.randint(key_of[3], (D, FF), 0, 16), jax.random.fold_in(key_of[3], 1), 0, 15).astype(jnp.int32),
        "zero_points": plant(jax.random.randint(key_of[4], (D, GROUPS), 0, 16), jax.random.fold_in(key_of[4], 1), 0, 15).astype(jnp.int32),
        "scales": jnp.clip(jnp.exp(math.log(0.003913119) - 1.3862944 * jax.random.uniform(key_of[5], (D, GROUPS), jnp.float32) ** steps_of(key_of[5], (D, GROUPS), ((0, 8), (1, 4)), -0.2, 0.2)), 0.0009782797, 0.003913119),
        "rotation": scatter_about(key_of[6], (BLOCK, BLOCK), BLOCK ** -0.5, 0.15625),
    }


def sylvester(order_size):
    indices = jnp.arange(order_size, dtype=jnp.int32)
    common_bits = indices[:, None] & indices[None, :]
    parity = jnp.zeros((order_size, order_size), jnp.int32)
    for bit_number in range(order_size.bit_length()):
        parity = parity + ((common_bits >> bit_number) & 1)
    return (1 - 2 * (parity % 2)).astype(jnp.float32)


def apply_hadamard(blocks):
    hadamard = sylvester(HAD)
    values = blocks.astype(jnp.float32).reshape(TOKENS, HAD, BLOCK)
    mixed = jnp.einsum("tab,ac->tcb", values, hadamard, precision=lax.Precision.HIGHEST)
    return (mixed * (1.0 / HAD ** 0.5)).astype(jnp.bfloat16).reshape(TOKENS, FF)


def reference(out_grad, gate_act, up_act, codes, zero_points, scales, rotation):
    gate32 = gate_act.astype(jnp.float32)
    up32 = up_act.astype(jnp.float32)
    sigmoid_gate = jax.nn.sigmoid(gate32)
    hidden = (gate32 * sigmoid_gate * up32).astype(jnp.bfloat16)
    mixed = jnp.dot(hidden.reshape(TOKENS * HAD, BLOCK), rotation, preferred_element_type=jnp.float32)
    mixed = mixed.astype(jnp.bfloat16).reshape(TOKENS, FF)
    rotated = apply_hadamard(mixed)
    levels = (codes.reshape(D, GROUPS, GROUP) - zero_points[:, :, None]).astype(jnp.float32)
    weight = (levels * scales[:, :, None]).astype(jnp.bfloat16).reshape(D, FF)
    grad_rotated = jnp.dot(out_grad, weight, preferred_element_type=jnp.float32).astype(jnp.bfloat16)
    grad_mixed = apply_hadamard(grad_rotated)
    grad_hidden = lax.dot_general(grad_mixed.reshape(TOKENS * HAD, BLOCK), rotation, (((1,), (1,)), ((), ())), preferred_element_type=jnp.float32)
    grad_hidden = grad_hidden.reshape(TOKENS, FF)
    grad_gate = (grad_hidden * up32 * sigmoid_gate * (1.0 + gate32 * (1.0 - sigmoid_gate))).astype(jnp.bfloat16)
    grad_up = (grad_hidden * gate32 * sigmoid_gate).astype(jnp.bfloat16)
    weight_grad = lax.dot_general(out_grad, rotated, (((0,), (0,)), ((), ())), preferred_element_type=jnp.float32)
    log_scale_grad = jnp.sum(weight_grad.reshape(D, GROUPS, GROUP) * levels, axis=2) * scales
    return grad_gate, grad_up, log_scale_grad
```

```python
import functools
import math

import jax
import jax.numpy as jnp
from jax import lax
from jax.experimental import pallas as pl
from jax.experimental.pallas import tpu as pltpu
from jax.sharding import PartitionSpec as P


F32 = jnp.float32
BF16 = jnp.bfloat16
LANES = 128


def pair_route(count):
    return [(i, i ^ 1) for i in range(count)]


def from_partner(block, axis, bit):
    count = lax.axis_size(axis)
    route = []
    for low in range(count):
        high = low | 1 << bit
        if high != low and high < count:
            route += [(low, high), (high, low)]
    return lax.ppermute(block, axis, route)


def cross_step(block, axis, bit):
    partner = from_partner(block.astype(BF16), axis, bit).astype(F32)
    own = block.astype(F32)
    high = lax.axis_index(axis) >> bit & 1 == 1
    return jnp.where(high, partner - own, own + partner)


def local_hadamard(parts):
    parts = list(parts)
    stride = 1
    while stride < len(parts):
        for i in range(len(parts)):
            if not i & stride:
                a, b = parts[i], parts[i | stride]
                parts[i], parts[i | stride] = a + b, a - b
        stride *= 2
    return parts


def levels_kernel(first_ref, codes_ref, zeros_ref, out_ref, *, group):
    tiles = codes_ref.shape[1] // LANES
    per_tile = LANES // group
    base = (first_ref[0] + pl.program_id(0)) * tiles
    for tile in range(tiles):
        turned = codes_ref[:, tile * LANES : (tile + 1) * LANES].astype(F32).T
        for g in range(per_tile):
            zero = zeros_ref[pl.ds((base + tile) * per_tile + g, 1), :].astype(F32)
            out_ref[tile * LANES + g * group : tile * LANES + (g + 1) * group, :] = (
                turned[g * group : (g + 1) * group, :] - zero
            ).astype(BF16)


def levels_of(codes, zeros_t, first, width, unit, group):
    rows = codes.shape[0]
    if unit % LANES or LANES % group:
        part = lax.dynamic_slice_in_dim(codes, first * unit, width, 1).T
        zero = lax.dynamic_slice_in_dim(zeros_t, first * (unit // group), width // group, 0)
        part = part.reshape(width // group, group, rows) - zero[:, None, :]
        return part.astype(BF16).reshape(width, rows)
    return pl.pallas_call(
        functools.partial(levels_kernel, group=group),
        out_shape=jax.ShapeDtypeStruct((width, rows), BF16),
        grid_spec=pltpu.PrefetchScalarGridSpec(
            num_scalar_prefetch=1,
            grid=(width // unit,),
            in_specs=[
                pl.BlockSpec((rows, unit), lambda j, first: (0, first[0] + j)),
                pl.BlockSpec(zeros_t.shape, lambda j, first: (0, 0)),
            ],
            out_specs=pl.BlockSpec((unit, rows), lambda j, first: (j, 0)),
        ),
        cost_estimate=pl.CostEstimate(
            flops=rows * width, bytes_accessed=6 * rows * width, transcendentals=0
        ),
    )(first.reshape(1).astype(jnp.int32), codes, zeros_t)


def on_device(out_grad, gate_act, up_act, codes, zero_points, scales, rotation):
    tok, columns = gate_act.shape
    block = rotation.shape[0]
    rows = codes.shape[0]
    groups = scales.shape[1]
    group = columns // groups
    local_blocks = columns // block
    dp = lax.axis_size("dp")
    tensor = lax.axis_size("tensor")
    bits = tensor.bit_length() - 1
    norm = 1.0 / math.sqrt(tensor * local_blocks)

    q = 2 if dp % 2 == 0 and local_blocks % 2 == 0 and groups % 2 == 0 else 1
    n = dp // q
    half = columns // q
    hgroups = groups // q
    me = lax.axis_index("dp")
    z = me // q
    p = me % q
    unit = 5 * LANES if half % (5 * LANES) == 0 else half
    units = half // unit
    if units == 5:
        chunks = [2, 3]
    else:
        chunks = [units]
    starts = [sum(chunks[:i]) for i in range(len(chunks))]

    def swap_pair(x):
        return lax.ppermute(x, "dp", pair_route(dp))

    def on_line(x, pairs):
        return lax.ppermute(
            x, "dp", [(a * q + k, b * q + k) for a, b in pairs for k in range(q)]
        )

    zeros_t = zero_points.T
    scales_t = scales.T

    kept, came = [], []
    for start, count in zip(starts, chunks):
        if q == 2:
            out = levels_of(codes, zeros_t, (1 - p) * units + start, count * unit, unit, group)
            came.append(swap_pair(out))
    for start, count in zip(starts, chunks):
        kept.append(levels_of(codes, zeros_t, p * units + start, count * unit, unit, group))
    scale_halves = scales_t.reshape(q, hgroups, rows)
    scale_kept = lax.dynamic_index_in_dim(scale_halves, p, 0, False)
    if q == 2:
        scale_came = swap_pair(lax.dynamic_index_in_dim(scale_halves, 1 - p, 0, False))

    split = 2 if tensor % 2 == 0 and tok % 32 == 0 else 1
    part = tok // split
    if split == 2:
        low = lax.axis_index("tensor") & 1
        mine = lax.dynamic_slice_in_dim(out_grad, low * part, part, 0)
    else:
        mine = out_grad
    wide = q * rows
    slots = []
    for s in range(n):
        piece = lax.dynamic_slice_in_dim(mine, (z + s) % n * wide, wide, 1)
        if s:
            piece = on_line(piece, [(a, (a + s) % n) for a in range(n)])
        slots.append(piece)
    g = jnp.stack(slots)[:, None]
    if q == 2:
        g = jnp.concatenate([g, swap_pair(g)], axis=1)
    if split == 2:
        other = from_partner(g, "tensor", 0)
        first_low = jnp.concatenate([g, other], axis=2)
        first_high = jnp.concatenate([other, g], axis=2)
        g = jnp.where(low == 0, first_low, first_high)
    g = g.reshape(n * q * tok, wide)
    if q == 2:
        swapped = jnp.concatenate([g[:, rows:], g[:, :rows]], axis=1)
        g = jnp.where(p == 0, g, swapped)

    gate32 = gate_act.astype(F32)
    up32 = up_act.astype(F32)
    sigmoid_gate = jax.nn.sigmoid(gate32)
    hidden = (gate32 * sigmoid_gate * up32).astype(BF16)
    stacked = jnp.concatenate(
        [hidden[:, a * block : (a + 1) * block] for a in range(local_blocks)], axis=0
    )
    mixed = jnp.dot(stacked, rotation, preferred_element_type=F32).astype(BF16)
    mixed = jnp.stack(
        [
            jnp.concatenate(
                [
                    mixed[a * tok : (a + 1) * tok]
                    for a in range(h * local_blocks // q, (h + 1) * local_blocks // q)
                ],
                axis=1,
            )
            for h in range(q)
        ]
    )
    crossed = mixed
    for bit in reversed(range(bits)):
        crossed = cross_step(crossed, "tensor", bit)

    def blocks_of(x):
        return [
            x[h][:, a * block : (a + 1) * block] for h in range(q) for a in range(local_blocks // q)
        ]

    rotated = [(v * norm).astype(BF16) for v in local_hadamard(blocks_of(crossed))]
    rotated = jnp.stack(
        [
            jnp.concatenate(rotated[h * local_blocks // q : (h + 1) * local_blocks // q], axis=1)
            for h in range(q)
        ]
    )
    r_kept = lax.dynamic_index_in_dim(rotated, p, 0, True)
    if q == 2:
        r_came = swap_pair(lax.dynamic_index_in_dim(rotated, 1 - p, 0, True))
        r_kept = jnp.concatenate([r_kept, r_came], axis=0)
    r_kept = r_kept.reshape(q * tok, half)

    def scaled(levels, scale):
        count = levels.shape[0] // group
        levels = levels.reshape(count, group, rows).astype(F32)
        return (levels * scale[:, None, :]).astype(BF16).reshape(count * group, rows)

    arrived = []
    for k, (start, count) in enumerate(zip(starts, chunks)):
        at, width = start * unit // group, count * unit // group
        weight = scaled(kept[k], scale_kept[at : at + width])
        if q == 2:
            weight = jnp.concatenate(
                [weight, scaled(came[k], scale_came[at : at + width])], axis=1
            )
        partial = lax.dot_general(
            g, weight, (((1,), (1,)), ((), ())), preferred_element_type=F32
        ).reshape(n, q * tok, count * unit)
        up = down = None
        for s in range(1, n):
            send = partial[s] if up is None else partial[s] + up.astype(F32)
            up = on_line(send.astype(BF16), [(a, a + 1) for a in range(s)])
            send = partial[n - s] if down is None else partial[n - s] + down.astype(F32)
            down = on_line(send.astype(BF16), [(a, a - 1) for a in range(n - s, n)])
        total = partial[0]
        if n > 1:
            total = total + up.astype(F32) + down.astype(F32)
        total = total.astype(BF16).reshape(q, tok, count * unit)
        if q == 2:
            other = swap_pair(total[1])
            total = jnp.where(
                p == 0, jnp.stack([total[0], other]), jnp.stack([other, total[0]])
            )
        for bit in reversed(range(bits)):
            total = cross_step(total, "tensor", bit)
        arrived.append(total)
    crossed_back = jnp.concatenate(arrived, axis=2)
    grad_mixed = [(v * norm).astype(BF16) for v in local_hadamard(blocks_of(crossed_back))]
    grad_hidden = lax.dot_general(
        jnp.concatenate(grad_mixed, axis=0),
        rotation,
        (((1,), (1,)), ((), ())),
        preferred_element_type=F32,
    )
    grad_hidden = jnp.concatenate(
        [grad_hidden[a * tok : (a + 1) * tok] for a in range(local_blocks)], axis=1
    )
    grad_gate = (grad_hidden * up32 * sigmoid_gate * (1.0 + gate32 * (1.0 - sigmoid_gate))).astype(
        BF16
    )
    grad_up = (grad_hidden * gate32 * sigmoid_gate).astype(BF16)

    sums = []
    for k, (start, count) in enumerate(zip(starts, chunks)):
        own = r_kept[:, start * unit : (start + count) * unit]
        ups, downs = [own], [own]
        for s in range(1, n):
            ups.append(on_line(ups[-1], [(a, a + 1) for a in range(s - 1, n - 1)]))
            downs.append(on_line(downs[-1], [(a, a - 1) for a in range(1, n - s + 1)]))
        gathered = jnp.concatenate(
            [own] + [jnp.where(z >= s, ups[s], downs[n - s]) for s in range(1, n)], axis=0
        )
        grad = lax.dot_general(
            gathered, g, (((0,), (0,)), ((), ())), preferred_element_type=F32
        )
        width = count * unit // group
        grad = grad.reshape(width, group, q, rows)
        levels = [kept[k]] + ([came[k]] if q == 2 else [])
        sums.append(
            jnp.stack(
                [
                    jnp.sum(grad[:, :, j] * levels[j].reshape(width, group, rows).astype(F32), axis=1)
                    for j in range(q)
                ]
            )
        )
    sums = jnp.concatenate(sums, axis=1)
    if q == 2:
        other = swap_pair(sums[1])
        sums = jnp.where(p == 0, jnp.stack([sums[0], other]), jnp.stack([other, sums[0]]))
    log_scale_grad = (sums.reshape(groups, rows) * scales_t).T
    return (grad_gate, grad_up, log_scale_grad)


def solution(mesh):
    return jax.shard_map(
        on_device,
        mesh=mesh,
        in_specs=(
            P("dp", None),
            P("dp", "tensor"),
            P("dp", "tensor"),
            P("dp", "tensor"),
            P("dp", "tensor"),
            P("dp", "tensor"),
            P(),
        ),
        out_specs=(P("dp", "tensor"), P("dp", "tensor"), P("dp", "tensor")),
        check_vma=False,
    )
```
